128 devices in a mesh: prow: 8 (over y, core), pcol: 16 (over x, z).
Axes of the slice: x: 4, y: 4, z: 4, core: 2. Of those that a mesh axis runs over, the one named last changes fastest.
Arguments:
- cross_cov: float32 [2, 512, 16384], P(None, 'prow', 'pcol'), may hold values from -6 to 6
- prev_rows: bfloat16 [2, 512, 32768], P(None, 'pcol', 'prow'), may hold values from -0.046875 to 0.046875
- prev_solved: bfloat16 [32768, 16384], P('prow', 'pcol'), may hold values from -6 to 6
- sub_block: float32 [512, 512], replicated, may hold values from -0.25 to 0.25
- inv_first: float32 [512, 512], replicated, as said below
- inv_second: float32 [512, 512], replicated, as said below
Outputs:
- solved: float32 [2, 512, 16384], P(None, 'prow', 'pcol')
The draws below stay inside these ranges and needn't reach their ends.
Inputs may be any that keep to these rules, and one draw needn't show every extreme that they name: inv_first is lower triangular with a positive diagonal. inv_second is lower triangular with a positive diagonal.
All inputs are finite; a program needn't handle non-finite values.
Results may differ from the reference program's by a relative error of at most 0.0003.
Values may be sent and summed in bfloat16 or wider, within the bound.
A program may use at most 64 MiB of HBM per device.

```python
import math
import jax
import jax.numpy as jnp
from jax import lax

NB = 512
R = 16384
PREV = 32768


def lower_inverse(key):
    first_key, second_key = jax.random.split(key)
    diagonal = jnp.exp(jax.random.uniform(first_key, (NB,), jnp.float32, math.log(0.5), math.log(2.0)))
    off_part = jax.random.normal(second_key, (NB, NB), jnp.float32)
    off_part = off_part * (1.0 / math.sqrt(NB))
    return jnp.tril(off_part, -1) + jnp.diag(diagonal)


def draw_inv_first(key, part):
    return lower_inverse(jax.random.fold_in(key, 11))


def draw_inv_second(key, part):
    return lower_inverse(jax.random.fold_in(key, 23))


def strengthened(result, key, source, target, blocks, factor):
    owner, partner = [(jnp.arange(result.shape[position]) // (result.shape[position] // blocks)).reshape([-1 if axis == position else 1 for axis in range(result.ndim)]) for position in (source, target)]
    chosen = jax.random.permutation(key, blocks)[partner]
    strong = (owner == chosen) | (owner == (partner + blocks // 2) % blocks)
    return jnp.where(strong, factor * result, result)


def level_of(stream_key, extent, pieces, least, top_value):
    factor_of = 1.0
    for dim, shards_of in pieces:
        draws = jax.random.uniform(jax.random.fold_in(jax.random.fold_in(stream_key, 6), dim), (shards_of,), jnp.float32, least / len(pieces), top_value / len(pieces))
        factor_of = factor_of * jnp.repeat(jnp.exp(draws), extent[dim] // shards_of).reshape((-1,) + (1,) * (len(extent) - 1 - dim))
    return factor_of


def bell_draw(rng, shape, width, limit, cuts=(), kind=jnp.bfloat16):
    values = jax.random.normal(rng, shape, jnp.float32) * width
    if len(cuts) > 0:
        values = level_of(rng, shape, cuts, -0.22, 0.18) * values
    return jnp.clip(values, min=-limit, max=limit).astype(kind)


def noise_with(stream_key, extent, scale, bound, shards, heavy, kind=jnp.bfloat16):
    drawn = scale * jax.random.normal(stream_key, extent, jnp.float32)
    if shards:
        drawn = drawn * level_of(stream_key, extent, shards, -0.22, 0.18)
    return jnp.clip(strengthened(drawn, jax.random.fold_in(stream_key, 3), *heavy), -bound, bound).astype(kind)


def setup_inputs(seed: int = 0) -> dict:
    seeds = jax.random.split(jax.random.key(seed), 7)
    return {
        "cross_cov": bell_draw(seeds[0], (2, NB, R), 1.0, 6.0, ((1, 8), (2, 16)), jnp.float32),
        "prev_rows": noise_with(seeds[1], (2, NB, PREV), PREV ** -0.5, 0.046875, ((1, 16), (2, 8)), (2, 1, 16, 2.0)),
        "prev_solved": bell_draw(seeds[2], (PREV, R), 1.0, 6.0, ((0, 8), (1, 16))),
        "sub_block": bell_draw(seeds[3], (NB, NB), NB ** -0.5, 0.25, (), jnp.float32),
        "inv_first": draw_inv_first(jax.random.fold_in(seeds[6], 71), 0),
        "inv_second": draw_inv_second(jax.random.fold_in(seeds[6], 71), 0),
    }


def mult(left, right):
    return jnp.dot(left, right, preferred_element_type=jnp.float32, precision=lax.Precision.HIGHEST)


def reference(cross_cov, prev_rows, prev_solved, sub_block, inv_first, inv_second):
    update_first = jnp.dot(prev_rows[0], prev_solved, preferred_element_type=jnp.float32)
    update_second = jnp.dot(prev_rows[1], prev_solved, preferred_element_type=jnp.float32)
    first_part = cross_cov[0] - update_first
    second_part = cross_cov[1] - update_second
    solved_first = mult(inv_first, first_part)
    second_rhs = second_part - mult(sub_block, solved_first)
    solved_second = mult(inv_second, second_rhs)
    return jnp.stack([solved_first, solved_second])
```

```python
import jax
import jax.numpy as jnp
from jax import lax
from jax.sharding import PartitionSpec as P


def mult(left, right, precision=lax.Precision.HIGHEST):
    return jnp.dot(left, right, preferred_element_type=jnp.float32, precision=precision)


def local(cross_cov, prev_rows, prev_solved, sub_block, inv_first, inv_second):
    rows = cross_cov.shape[1]
    terms = jnp.einsum(
        "kra,ac->krc",
        lax.all_gather(prev_rows, "pcol", axis=1, tiled=True),
        prev_solved,
        preferred_element_type=jnp.float32,
    )
    offset = lax.axis_index("prow") * rows
    rhs = lax.dynamic_update_slice_in_dim(-terms, lax.dynamic_slice_in_dim(-terms, offset, rows, 1) + cross_cov, offset, 1)
    coupling = -mult(inv_second, mult(sub_block, inv_first))
    high = lax.Precision.HIGH
    nb = inv_first.shape[0]
    transform = jnp.concatenate([
        jnp.concatenate([inv_first, jnp.zeros_like(inv_first)], axis=1),
        jnp.concatenate([coupling, inv_second], axis=1),
    ])
    both = mult(transform, rhs.reshape(2 * nb, -1), high).reshape(rhs.shape)
    return lax.psum_scatter(both, "prow", scatter_dimension=1, tiled=True)


def solution(mesh):
    return jax.shard_map(
        local,
        mesh=mesh,
        in_specs=(
            P(None, "prow", "pcol"),
            P(None, "pcol", "prow"),
            P("prow", "pcol"),
            P(),
            P(),
            P(),
        ),
        out_specs=P(None, "prow", "pcol"),
        check_vma=False,
    )
```

```python
import jax
import jax.numpy as jnp
from jax import lax
from jax.sharding import PartitionSpec as P


def mult(left, right, precision=lax.Precision.HIGHEST):
    return jnp.dot(left, right, preferred_element_type=jnp.float32, precision=precision)


def local(cross_cov, prev_rows, prev_solved, sub_block, inv_first, inv_second):
    rows = cross_cov.shape[1]
    pieces = 2
    width = prev_rows.shape[2] // pieces
    terms = None
    for p in range(pieces):
        gathered = lax.all_gather(prev_rows[:, :, p * width:(p + 1) * width], "pcol", axis=1, tiled=True)
        part = jnp.einsum("kra,ac->krc", gathered, prev_solved[p * width:(p + 1) * width],
                          preferred_element_type=jnp.float32)
        terms = part if terms is None else terms + part
    offset = lax.axis_index("prow") * rows
    rhs = lax.dynamic_update_slice_in_dim(-terms, lax.dynamic_slice_in_dim(-terms, offset, rows, 1) + cross_cov, offset, 1)
    coupling = -mult(inv_second, mult(sub_block, inv_first))
    high = lax.Precision.HIGH
    nb = inv_first.shape[0]
    transform = jnp.concatenate([
        jnp.concatenate([inv_first, jnp.zeros_like(inv_first)], axis=1),
        jnp.concatenate([coupling, inv_second], axis=1),
    ])
    flat = rhs.reshape(2 * nb, -1)
    cols = flat.shape[1] // pieces
    out = []
    for p in range(pieces):
        both = mult(transform, flat[:, p * cols:(p + 1) * cols], high).reshape(2, nb, cols)
        out.append(lax.psum_scatter(both, "prow", scatter_dimension=1, tiled=True))
    return jnp.concatenate(out, axis=2)


def solution(mesh):
    return jax.shard_map(
        local,
        mesh=mesh,
        in_specs=(
            P(None, "prow", "pcol"),
            P(None, "pcol", "prow"),
            P("prow", "pcol"),
            P(),
            P(),
            P(),
        ),
        out_specs=P(None, "prow", "pcol"),
        check_vma=False,
    )
```

```python
import jax
import jax.numpy as jnp
from jax import lax
from jax.sharding import PartitionSpec as P


def mult(left, right):
    return jnp.dot(left, right, preferred_element_type=jnp.float32, precision=lax.Precision.HIGH)


def local(cross_cov, prev_rows, prev_solved, sub_block, inv_first, inv_second):
    rows = cross_cov.shape[1]
    terms = jnp.einsum(
        "kra,ac->krc",
        lax.all_gather(prev_rows, "pcol", axis=1, tiled=True),
        prev_solved,
        preferred_element_type=jnp.float32,
    )
    offset = lax.axis_index("prow") * rows
    rhs = lax.dynamic_update_slice_in_dim(-terms, lax.dynamic_slice_in_dim(-terms, offset, rows, 1) + cross_cov, offset, 1)
    first = mult(inv_first, rhs[0])
    second = mult(inv_second, rhs[1] - mult(sub_block, first))
    both = jnp.concatenate([first, second]).reshape((2,) + first.shape)
    return lax.psum_scatter(both, "prow", scatter_dimension=1, tiled=True)


def solution(mesh):
    return jax.shard_map(
        local,
        mesh=mesh,
        in_specs=(
            P(None, "prow", "pcol"),
            P(None, "pcol", "prow"),
            P("prow", "pcol"),
            P(),
            P(),
            P(),
        ),
        out_specs=P(None, "prow", "pcol"),
        check_vma=False,
    )
```
